32 devices in a mesh: row: 16 (over z, x, core), col: 2 (over y).
Axes of the slice: x: 2, y: 2, z: 4, core: 2. Of those that a mesh axis runs over, the one named last changes fastest.
Arguments:
- left_act: bfloat16 [512, 4096], P('row', 'col'), may hold values from -18 to 18
- right_act: bfloat16 [256, 4096], P('col', 'row'), may hold values from -18 to 18
- out_weight: bfloat16 [1024, 128], replicated, may hold values from -0.1875 to 0.1875
- out_bias: float32 [128], replicated, may hold values from -1 to 1
- pair_grad: bfloat16 [512, 256, 128], P('row', 'col'), may hold values from -13 to 13
Outputs:
- pair_out: bfloat16 [512, 256, 128], P('row', 'col')
- left_grad: float32 [512, 4096], P('row', 'col')
- right_grad: float32 [256, 4096], P('col', 'row')
- weight_grad: float32 [1024, 128], replicated
- bias_grad: float32 [128], replicated
The draws below stay inside these ranges and needn't reach their ends.
All inputs are finite; a program needn't handle non-finite values.
Results may differ from the reference program's by a relative error of at most 0.005.
Values may be sent and summed in bfloat16 or wider, within the bound.
A program may use at most 128 MiB of HBM per device.

```python
import jax
import jax.numpy as jnp
from jax import lax

S = 128
C = 32
CZ = 128
TR = 32
CC = 1024
LI = 512
LJ = 256


def draw_pair_grad(key, part):
    first, second = jax.random.split(jax.random.fold_in(key, 7), 2)
    base = jnp.clip(jax.random.normal(first, (LI, LJ, CZ), jnp.float32), -3.0, 3.0)
    rising = 3.0 ** (jnp.arange(LI, dtype=jnp.float32) / max(LI - 1, 1))
    noise = jax.random.uniform(second, (LI, 1, 1), jnp.float32, 0.7, 1.4)
    values = base
    return (values * rising[:, None, None] * noise).astype(jnp.bfloat16)


def level_of(stream_key, shape, shards, least, largest):
    def one(dim, shards_of):
        heights = jax.random.uniform(jax.random.fold_in(jax.random.fold_in(stream_key, 6), dim), (shards_of,), jnp.float32, least / len(shards), largest / len(shards))
        return jnp.repeat(jnp.exp(heights), shape[dim] // shards_of).reshape((-1,) + (1,) * (len(shape) - dim - 1))

    loudness = one(*shards[0])
    for cut in shards[1:]:
        loudness = loudness * one(*cut)
    return loudness


def normal_values(own_key, extent, spread, limit, cuts=(), kind=jnp.bfloat16):
    values = spread * jax.random.normal(own_key, extent, jnp.float32)
    if cuts:
        values = values * level_of(own_key, extent, cuts, -0.22, 0.18)
    return jnp.clip(values, -limit, limit).astype(kind)


def setup_inputs(seed: int = 0) -> dict:
    splits = jax.random.split(jax.random.key(seed), 6)
    left_act = normal_values(splits[0], (LI, S * C), 3.0, 18.0, ((0, 16), (1, 2)))
    right_act = normal_values(splits[1], (LJ, S * C), 3.0, 18.0, ((0, 2), (1, 16)))
    out_weight = normal_values(splits[2], (CC, CZ), CC ** -0.5, 0.1875)
    out_bias = jnp.clip(jax.random.uniform(splits[3], (CZ,), jnp.float32, -1.0, 1.0), -1.0, 1.0)
    pair_grad = draw_pair_grad(jax.random.fold_in(splits[5], 71), 0)
    return dict(left_act=left_act, right_act=right_act, out_weight=out_weight, out_bias=out_bias, pair_grad=pair_grad)


def reference(left_act, right_act, out_weight, out_bias, pair_grad):
    factor = 1.0 / S
    right_tiles = right_act.astype(jnp.float32).reshape(LJ, S, C)
    left_blocks = left_act.astype(jnp.float32).reshape(LI // TR, TR, S, C)
    grad_blocks = pair_grad.reshape(LI // TR, TR, LJ, CZ)

    def advance(carry, inputs):
        weight_sum, bias_sum, right_sum = carry
        left_block, grad_block = inputs
        outer = (jnp.einsum('isc,jsd->ijcd', left_block, right_tiles) * factor).astype(jnp.bfloat16).reshape(TR * LJ, C * C)
        pre = jnp.dot(outer, out_weight, preferred_element_type=jnp.float32) + out_bias
        sigmoid_pre = jax.nn.sigmoid(pre)
        pair_block = (pre * sigmoid_pre).astype(jnp.bfloat16)
        slope = sigmoid_pre * (1.0 + pre * (1.0 - sigmoid_pre))
        dpre = (grad_block.reshape(TR * LJ, CZ).astype(jnp.float32) * slope).astype(jnp.bfloat16)
        weight_sum = weight_sum + jnp.dot(outer.T, dpre, preferred_element_type=jnp.float32)
        bias_sum = bias_sum + jnp.sum(dpre.astype(jnp.float32), axis=0)
        douter = jnp.dot(dpre, out_weight.T, preferred_element_type=jnp.float32).astype(jnp.bfloat16)
        douter = lax.optimization_barrier(douter).astype(jnp.float32).reshape(TR, LJ, C, C)
        left_block_grad = jnp.einsum('ijcd,jsd->isc', douter, right_tiles) * factor
        right_sum = right_sum + jnp.einsum('ijcd,isc->jsd', douter, left_block) * factor
        return (weight_sum, bias_sum, right_sum), (pair_block.reshape(TR, LJ, CZ), left_block_grad.reshape(TR, S * C))

    initial = (jnp.zeros((C * C, CZ), jnp.float32), jnp.zeros((CZ,), jnp.float32), jnp.zeros((LJ, S, C), jnp.float32))
    carry, outputs = lax.scan(advance, initial, (left_blocks, grad_blocks))
    weight_sum, bias_sum, right_sum = carry
    pair_blocks, left_rows = outputs
    return (pair_blocks.reshape(LI, LJ, CZ), left_rows.reshape(LI, S * C), right_sum.reshape(LJ, S * C), weight_sum / LI, bias_sum / LI)
```

```python
import functools

import jax
import jax.numpy as jnp
from jax import lax
from jax.experimental import pallas as pl
from jax.experimental.pallas import tpu as pltpu
from jax.sharding import PartitionSpec as P

S = 128
C = 32
CZ = 128
MESH = pl.DeviceIdType.MESH
BF = jnp.bfloat16
F32 = jnp.float32
PAD = 16


def place():
    r = lax.axis_index("row")
    return r // 4, (r // 2) % 2, r % 2, lax.axis_index("col")


def row_of(o, x, k):
    return o * 4 + x * 2 + k


def greet(n, cn):
    o, x, k, y = place()
    barrier = pltpu.get_barrier_semaphore()
    peers = [(row_of(lax.rem(o + t, n), x, k), y) for t in range(1, n)]
    peers += [(row_of(o, 1 - x, k), y), (row_of(o, x, 1 - k), y)]
    peers += [(row_of(o, x, k), lax.rem(y + t, cn)) for t in range(1, cn)]
    for peer in peers:
        pl.semaphore_signal(barrier, inc=1, device_id=peer, device_id_type=MESH)
    pl.semaphore_wait(barrier, len(peers))


def remote(src, dst, send, recv, peer):
    return pltpu.make_async_remote_copy(
        src_ref=src, dst_ref=dst, send_sem=send, recv_sem=recv, device_id=peer, device_id_type=MESH
    )


def spread(n, buf, sems):
    o, x, k, y = place()
    zs, zr, xs, xr, cs, cr = sems
    started = []

    def send(slot, ss, rs, peer):
        copy = remote(buf.at[slot], buf.at[slot], ss, rs, peer)
        copy.start()
        started.append(copy)
        return copy

    xpeer, cpeer = (row_of(o, 1 - x, k), y), (row_of(o, x, 1 - k), y)
    own = (k, x, o)
    zc = {
        t: send(own, zs.at[t], zr.at[t], (row_of(lax.rem(o + t, n), x, k), y)) for t in range(1, n)
    }
    xc = [send(own, xs.at[0], xr.at[0], xpeer)]
    cc = [send(own, cs.at[0], cr.at[0], cpeer)]
    for t in range(1, n):
        zc[t].wait_recv()
        slot = (k, x, lax.rem(o - t + n, n))
        xc.append(send(slot, xs.at[t], xr.at[t], xpeer))
        cc.append(send(slot, cs.at[t], cr.at[t], cpeer))
    for t in range(n):
        xc[t].wait_recv()
        slot = (k, 1 - x, lax.rem(o - t + n, n))
        cc.append(send(slot, cs.at[n + t], cr.at[n + t], cpeer))
    for copy in cc:
        copy.wait_recv()
    for copy in started:
        copy.wait_send()


def spread_sems(n):
    dma = pltpu.SemaphoreType.DMA
    return [dma((n,)), dma((n,)), dma((n,)), dma((n,)), dma((2 * n,)), dma((2 * n,))]


def gather_kernel(n, cn, a_ref, b_ref, a_all, b_all, ysend, yrecv, *sems):
    o, x, k, y = place()
    b_all[k, x, o] = b_ref[...]
    a_all[y] = a_ref[...]
    greet(n, cn)
    ac = []
    for t in range(1, cn):
        copy = remote(
            a_ref, a_all.at[y], ysend.at[t], yrecv.at[t],
            (row_of(o, x, k), lax.rem(y + t, cn)),
        )
        copy.start()
        ac.append(copy)
    spread(n, b_all, sems)
    for copy in ac:
        copy.wait()


def gather(n, cn, a_loc, b_loc):
    dma = pltpu.SemaphoreType.DMA
    vmem = pl.BlockSpec(memory_space=pltpu.VMEM)
    return pl.pallas_call(
        functools.partial(gather_kernel, n, cn),
        out_shape=(
            jax.ShapeDtypeStruct((cn,) + a_loc.shape, BF),
            jax.ShapeDtypeStruct((2, 2, n) + b_loc.shape, BF),
        ),
        in_specs=[vmem] * 2,
        out_specs=(vmem, vmem),
        scratch_shapes=[dma((cn,)), dma((cn,))] + spread_sems(n),
        compiler_params=pltpu.CompilerParams(collective_id=0, has_side_effects=True),
        name="gather",
    )(a_loc, b_loc)


def dot(a, b):
    return jnp.dot(a, b, preferred_element_type=F32)


def compute_kernel(
    n, cn, ti, tj, a_ref, b_ref, w_ref, wt_ref, bias_ref, pg_ref,
    po_ref, lp_ref, rp_ref, wp_ref,
    b_f, b_s, bt_s, at_s, a_s, ot_s, dt_s, d_s, wg_s, lg_s, bg_s,
):
    factor = 1.0 / S
    cc = C * C
    rows = 4 * n
    sr, sc = S // rows, S // cn
    group = min(8, ti)
    gc, gj = group * C, group * tj
    groups = ti // group
    dq = 8
    quarters = C // dq
    for o in range(n):
        for x in range(2):
            for k in range(2):
                b_f[pl.ds(row_of(o, x, k) * sr, sr), :] = b_ref[k, x, o].astype(F32)
    for q in range(quarters):
        cols = slice(q * dq * tj, (q + 1) * dq * tj)
        part = b_f[:, cols]
        b_s[:, cols] = part.astype(BF)
        bt_s[cols, :] = part.T.astype(BF)
    for y in range(cn):
        a_s[y * sc : (y + 1) * sc, :] = (a_ref[y].astype(F32) * factor).astype(BF)
    at_s[...] = a_s[...].astype(F32).T.astype(BF)
    wg_s[...] = jnp.zeros_like(wg_s)
    bg_s[...] = jnp.zeros_like(bg_s)
    lg_s[...] = jnp.zeros_like(lg_s)
    bias = bias_ref[...]

    def forward(g, carry):
        at = at_s[pl.ds(pl.multiple_of(g * gc, gc), gc), :]
        for q in range(quarters):
            res = dot(at, b_s[:, q * dq * tj : (q + 1) * dq * tj]).astype(BF)
            for i in range(group):
                for d in range(dq):
                    dd = q * dq + d
                    ot_s[dd * C : (dd + 1) * C, i * tj : (i + 1) * tj] = res[
                        i * C : (i + 1) * C, d * tj : (d + 1) * tj
                    ]
        pre = dot(wt_ref[...], ot_s[...]).T + bias
        sig = jax.nn.sigmoid(pre)
        first = pl.ds(pl.multiple_of(g * group, group), group)
        po_ref[first] = (pre * sig).astype(BF).reshape(group, tj, CZ)
        slope = sig * (1.0 + pre * (1.0 - sig))
        pg = pg_ref[first].reshape(gj, CZ).astype(F32)
        dpre = (pg * slope).astype(BF)
        dpre_f = dpre.astype(F32)
        bg_s[...] += jnp.sum(dpre_f.reshape(gj // 8, 8, CZ), axis=0)
        dt_s[g] = dpre_f.T.astype(BF)
        wg_s[...] += dot(ot_s[...], dpre)
        return carry

    lax.fori_loop(0, groups, forward, 0)

    def backward(q, carry):
        wq = w_ref[pl.ds(pl.multiple_of(q * dq * C, dq * C), dq * C), :]
        for g in range(groups):
            res = dot(wq, dt_s[g]).astype(BF)
            for i in range(group):
                for d in range(dq):
                    d_s[g * gc + i * C : g * gc + (i + 1) * C, d * tj : (d + 1) * tj] = res[
                        d * C : (d + 1) * C, i * tj : (i + 1) * tj
                    ]
        cols = pl.ds(pl.multiple_of(q * dq * tj, dq * tj), dq * tj)
        right = dot(a_s[...], d_s[...])
        for o in range(n):
            for x in range(2):
                for k in range(2):
                    r = row_of(o, x, k) * sr
                    rp_ref[k, x, o, :, cols] = right[r : r + sr].astype(BF)
        lg_s[...] += dot(d_s[...], bt_s[cols, :])
        return carry

    lax.fori_loop(0, quarters, backward, 0)
    left = lg_s[...].T * factor
    for y in range(cn):
        lp_ref[y] = left[y * sc : (y + 1) * sc].astype(BF)
    wr = cc // rows
    bias_rows = jnp.broadcast_to(jnp.sum(bg_s[...], axis=0, keepdims=True), (PAD, CZ)).astype(BF)
    for o in range(n):
        for x in range(2):
            for k in range(2):
                r = row_of(o, x, k) * wr
                wp_ref[k, x, o, 0:wr, :] = wg_s[r : r + wr, :].astype(BF)
                wp_ref[k, x, o, wr : wr + PAD, :] = bias_rows


def compute(n, cn, a_all, b_all, w, wt, bias, pg):
    ti, tj = pg.shape[:2]
    rows = 4 * n
    cc = C * C
    group = min(8, ti)
    vmem = pl.BlockSpec(memory_space=pltpu.VMEM)
    return pl.pallas_call(
        functools.partial(compute_kernel, n, cn, ti, tj),
        out_shape=(
            jax.ShapeDtypeStruct(pg.shape, BF),
            jax.ShapeDtypeStruct((cn, S // cn, ti * C), BF),
            jax.ShapeDtypeStruct((2, 2, n, S // rows, C * tj), BF),
            jax.ShapeDtypeStruct((2, 2, n, cc // rows + PAD, CZ), BF),
        ),
        in_specs=[vmem] * 6,
        out_specs=(vmem,) * 4,
        scratch_shapes=[
            pltpu.VMEM((S, C * tj), F32),
            pltpu.VMEM((S, C * tj), BF),
            pltpu.VMEM((C * tj, S), BF),
            pltpu.VMEM((ti * C, S), BF),
            pltpu.VMEM((S, ti * C), BF),
            pltpu.VMEM((cc, group * tj), BF),
            pltpu.VMEM((ti // group, CZ, group * tj), BF),
            pltpu.VMEM((ti * C, 8 * tj), BF),
            pltpu.VMEM((cc, CZ), F32),
            pltpu.VMEM((ti * C, S), F32),
            pltpu.VMEM((8, CZ), F32),
        ],
        compiler_params=pltpu.CompilerParams(vmem_limit_bytes=60 * 1024 * 1024),
        name="pairs",
    )(a_all, b_all, w, wt, bias, pg)


def reduce_kernel(
    n, cn, scale, lp, rp, wp, lo_ref, ro_ref, wo_ref,
    lbuf, rc, rs1, rx, rs2, rz, wc, ws1, wx, ws2, wz, wy,
    lss, lsr, ycs, ycr,
    rcs, rcr, rxs, rxr, rzs, rzr, wcs, wcr, wxs, wxr, wzs, wzr, *gsems,
):
    o, x, k, y = place()
    xpeer, cpeer = (row_of(o, 1 - x, k), y), (row_of(o, x, 1 - k), y)
    greet(n, cn)
    pending = []

    def go(src, dst, ss, rs, peer):
        copy = remote(src, dst, ss, rs, peer)
        copy.start()
        pending.append(copy)
        return copy

    order = list(range(1, n)) + [0]
    wcore, rcore = {}, {}
    for side in range(2):
        for t in order:
            xx = 1 - x if side == 0 else x
            oo = lax.rem(o + t, n)
            at = side * n + t
            wcore[at] = go(
                wp.at[1 - k, xx, oo], wc.at[at], wcs.at[at], wcr.at[at], cpeer
            )
    for side in range(2):
        for t in order:
            xx = 1 - x if side == 0 else x
            oo = lax.rem(o + t, n)
            at = side * n + t
            rcore[at] = go(
                rp.at[1 - k, xx, oo], rc.at[at], rcs.at[at], rcr.at[at], cpeer
            )
    lefts = [
        go(
            lp.at[lax.rem(y + t, cn)], lbuf.at[t], lss.at[t], lsr.at[t],
            (row_of(o, x, k), lax.rem(y + t, cn)),
        )
        for t in range(1, cn)
    ]

    def level_x(part, cbuf, core, s1, xbuf, sends, recvs):
        copies = {}
        for t in order:
            core[t].wait_recv()
            s1[t] = (
                part[k, 1 - x, lax.rem(o + t, n)].astype(F32) + cbuf[t].astype(F32)
            ).astype(BF)
            copies[t] = go(s1.at[t], xbuf.at[t], sends.at[t], recvs.at[t], xpeer)
        return copies

    def level_z(part, cbuf, core, xcopies, xbuf, s2, zbuf, sends, recvs):
        copies = {}
        for t in order:
            core[n + t].wait_recv()
            xcopies[t].wait_recv()
            total = (
                part[k, x, lax.rem(o + t, n)].astype(F32)
                + cbuf[n + t].astype(F32)
                + xbuf[t].astype(F32)
            )
            if t == 0:
                return copies, total
            s2[t] = total.astype(BF)
            copies[t] = go(
                s2.at[t], zbuf.at[t], sends.at[t], recvs.at[t],
                (row_of(lax.rem(o + t, n), x, k), y),
            )

    def finish(total, copies, zbuf):
        for t in range(1, n):
            copies[t].wait_recv()
            total = total + zbuf[t].astype(F32)
        return total

    wxc = level_x(wp, wc, wcore, ws1, wx, wxs, wxr)
    rxc = level_x(rp, rc, rcore, rs1, rx, rxs, rxr)
    wzc, wtot = level_z(wp, wc, wcore, wxc, wx, ws2, wz, wzs, wzr)
    rzc, rtot = level_z(rp, rc, rcore, rxc, rx, rs2, rz, rzs, rzr)
    ro_ref[...] = rtot
    wy[y] = finish(wtot, wzc, wz).astype(BF)
    ysum = [
        go(
            wy.at[y], wy.at[y], ycs.at[t], ycr.at[t],
            (row_of(o, x, k), lax.rem(y + t, cn)),
        )
        for t in range(1, cn)
    ]
    left = lp[y].astype(F32)
    for t in range(1, cn):
        lefts[t - 1].wait_recv()
        left = left + lbuf[t].astype(F32)
    lo_ref[...] = left
    for copy in ysum:
        copy.wait_recv()
    total = wy[0].astype(F32)
    for t in range(1, cn):
        total = total + wy[t].astype(F32)
    wo_ref[k, x, o] = (total * scale).astype(BF)
    spread(n, wo_ref, gsems)
    ro_ref[...] = finish(ro_ref[...], rzc, rz)
    for copy in pending:
        copy.wait_send()


def reduce(n, cn, scale, lp, rp, wp):
    dma = pltpu.SemaphoreType.DMA
    vmem = pl.BlockSpec(memory_space=pltpu.VMEM)
    rb, wb = rp.shape[3:], wp.shape[3:]

    def buffers(block):
        return [
            pltpu.VMEM((2 * n,) + block, BF),
            pltpu.VMEM((n,) + block, BF),
            pltpu.VMEM((n,) + block, BF),
            pltpu.VMEM((n,) + block, BF),
            pltpu.VMEM((n,) + block, BF),
        ]

    sems = [dma((2 * n,)), dma((2 * n,)), dma((n,)), dma((n,)), dma((n,)), dma((n,))]
    return pl.pallas_call(
        functools.partial(reduce_kernel, n, cn, scale),
        out_shape=(
            jax.ShapeDtypeStruct(lp.shape[1:], F32),
            jax.ShapeDtypeStruct(rb, F32),
            jax.ShapeDtypeStruct(wp.shape, BF),
        ),
        in_specs=[vmem] * 3,
        out_specs=(vmem,) * 3,
        scratch_shapes=[pltpu.VMEM(lp.shape, BF)]
        + buffers(rb)
        + buffers(wb)
        + [pltpu.VMEM((cn,) + wb, BF)]
        + [dma((cn,)), dma((cn,)), dma((cn,)), dma((cn,))]
        + sems
        + sems
        + spread_sems(n),
        compiler_params=pltpu.CompilerParams(collective_id=1, has_side_effects=True),
        name="reduce",
    )(lp, rp, wp)


def on_device(left_act, right_act, out_weight, out_bias, pair_grad):
    n, cn = lax.axis_size("row") // 4, lax.axis_size("col")
    rows = 4 * n
    ti, tj = left_act.shape[0], right_act.shape[0]
    sc, sr = S // cn, S // rows
    first_total = ti * rows
    a_loc = left_act.reshape(ti, sc, C).transpose(1, 0, 2).reshape(sc, ti * C)
    b_loc = right_act.T.reshape(sr, C * tj)
    w = out_weight.reshape(C, C, CZ).transpose(1, 0, 2).reshape(C * C, CZ)
    a_all, b_all = gather(n, cn, a_loc, b_loc)
    po, lp, rp, wp = compute(n, cn, a_all, b_all, w, w.T, out_bias.reshape(1, CZ), pair_grad)
    left, right, wsum = reduce(n, cn, 1.0 / first_total, lp, rp, wp)
    left_grad = left.reshape(sc, ti, C).transpose(1, 0, 2).reshape(ti, sc * C)
    right_grad = right.reshape(sr * C, tj).T
    wr = C * C // rows
    wsum = wsum.transpose(2, 1, 0, 3, 4).reshape(rows, wr + PAD, CZ)
    weight_grad = (
        wsum[:, :wr].reshape(C, C, CZ).transpose(1, 0, 2).reshape(C * C, CZ).astype(F32)
    )
    bias_grad = wsum[0, wr].astype(F32)
    return (po, left_grad, right_grad, weight_grad, bias_grad)


def solution(mesh):
    in_specs = (P("row", "col"), P("col", "row"), P(), P(), P("row", "col", None))
    out_specs = (P("row", "col", None), P("row", "col"), P("col", "row"), P(), P())
    return jax.shard_map(
        on_device, mesh=mesh, in_specs=in_specs, out_specs=out_specs, check_vma=False
    )
```

```python
import functools

import jax
import jax.numpy as jnp
from jax import lax
from jax.experimental import pallas as pl
from jax.experimental.pallas import tpu as pltpu
from jax.sharding import PartitionSpec as P

S = 128
C = 32
CZ = 128
MESH = pl.DeviceIdType.MESH
BF = jnp.bfloat16
F32 = jnp.float32
DQ = 8
QUARTERS = C // DQ


def dot(a, b):
    return jnp.dot(a, b, preferred_element_type=F32)


def flip(o, t):
    out, bit = 0, 1
    while bit <= t:
        here = (o // bit) % 2
        out = out + bit * ((1 - here) if (t & bit) else here)
        bit *= 2
    return out + (o // bit) * bit


def row_of(o, x, k):
    return o * 4 + x * 2 + k


def remote(src, dst, send, recv, peer):
    return pltpu.make_async_remote_copy(
        src_ref=src, dst_ref=dst, send_sem=send, recv_sem=recv, device_id=peer, device_id_type=MESH
    )


def spread(n, ids, buf, sems):
    o, x, k, y = ids
    zs, zr, xs, xr, cs, cr = sems
    started = []

    def send(slot, ss, rs, peer):
        copy = remote(buf.at[slot], buf.at[slot], ss, rs, peer)
        copy.start()
        started.append(copy)
        return copy

    xpeer, cpeer = (row_of(o, 1 - x, k), y), (row_of(o, x, 1 - k), y)
    own = (k, x, o)
    zc = {t: send(own, zs.at[t], zr.at[t], (row_of(flip(o, t), x, k), y)) for t in range(1, n)}
    xc = [send(own, xs.at[0], xr.at[0], xpeer)]
    cc = [send(own, cs.at[0], cr.at[0], cpeer)]
    yield
    for t in range(1, n):
        zc[t].wait_recv()
        slot = (k, x, flip(o, t))
        xc.append(send(slot, xs.at[t], xr.at[t], xpeer))
        cc.append(send(slot, cs.at[t], cr.at[t], cpeer))
    yield
    for t in range(n):
        xc[t].wait_recv()
        slot = (k, 1 - x, flip(o, t))
        cc.append(send(slot, cs.at[n + t], cr.at[n + t], cpeer))
    yield
    for copy in cc:
        copy.wait_recv()
    for copy in started:
        copy.wait_send()


def spread_sems(n):
    dma = pltpu.SemaphoreType.DMA
    return [dma((n,)), dma((n,)), dma((n,)), dma((n,)), dma((2 * n,)), dma((2 * n,))]


def kernel(
    n, cn, ti, tj, left_ref, right_ref, w_ref, bias_ref, pg_ref,
    po_ref, lo_ref, ro_ref, wo_ref, bo_ref,
    a_all, b_all, b_t, wide, w_f, w2_s, wt_s, at_f, at_s, a_s, b_f, b_s, bt_s,
    ot_s, dt_s, d_s, wg_s, lg_s, bg_s,
    rp, rc, rs1, rx, rs2, rz, rfin, lp, lbuf, wp, wc, ws1, wx, ws2, wz, wy, wall,
    asend, arecv, lsend, lrecv, ysend, yrecv,
    rcs, rcr, rxs, rxr, rzs, rzr, wcs, wcr, wxs, wxr, wzs, wzr, *spreads,
):
    r = lax.axis_index("row")
    o, x, k, y = r // 4, (r // 2) % 2, r % 2, lax.axis_index("col")
    ids = (o, x, k, y)
    xpeer, cpeer = (row_of(o, 1 - x, k), y), (row_of(o, x, 1 - k), y)
    opeer = {t: (row_of(flip(o, t), x, k), y) for t in range(1, n)}
    ypeer = {t: (r, lax.rem(y + t, cn)) for t in range(1, cn)}
    factor = 1.0 / S
    cc = C * C
    rows = 4 * n
    sr, sc, wr = S // rows, S // cn, cc // rows
    first_total = ti * rows
    group = min(8, ti)
    gc, gj = group * C, group * tj
    groups = ti // group
    qw = DQ * tj
    every = [(oo, xx, kk) for oo in range(n) for xx in range(2) for kk in range(2)]
    pending = []

    def go(src, dst, ss, rs, peer):
        copy = remote(src, dst, ss, rs, peer)
        copy.start()
        pending.append(copy)
        return copy

    barrier = pltpu.get_barrier_semaphore()
    peers = list(opeer.values()) + [xpeer, cpeer] + list(ypeer.values())
    for peer in peers:
        pl.semaphore_signal(barrier, inc=1, device_id=peer, device_id_type=MESH)
    b_t[...] = right_ref[...].astype(F32).T
    for d in range(C):
        b_all[k, x, o, :, d * tj : (d + 1) * tj] = b_t[pl.ds(d, sr, stride=C), :].astype(BF)
    pl.semaphore_wait(barrier, len(peers))
    ring = spread(n, ids, b_all, spreads[:6])
    next(ring)
    firsts = [
        go(left_ref, a_all.at[y], asend.at[t], arecv.at[t], ypeer[t]) for t in range(1, cn)
    ]
    a_all[y] = left_ref[...]
    w_f[...] = w_ref[...].astype(F32)
    for d in range(C):
        w2_s[d * C : (d + 1) * C, :] = w_f[pl.ds(d, C, stride=C), :].astype(BF)
    next(ring)
    wt_s[...] = w2_s[...].astype(F32).T.astype(BF)
    wg_s[...] = jnp.zeros_like(wg_s)
    bg_s[...] = jnp.zeros_like(bg_s)
    bias = bias_ref[...]
    for copy in firsts:
        copy.wait_recv()
    next(ring)
    for yy in range(cn):
        wide[yy * sc * C : (yy + 1) * sc * C, :] = a_all[yy].astype(F32).T
    for c in range(C):
        at_f[pl.ds(c, ti, stride=C), :] = wide[pl.ds(c, S, stride=C), :].T * factor
    at_s[...] = at_f[...].astype(BF)
    a_s[...] = at_f[...].T.astype(BF)
    for _ in ring:
        pass
    for oo, xx, kk in every:
        b_f[pl.ds(row_of(oo, xx, kk) * sr, sr), :] = b_all[kk, xx, oo].astype(F32)
    for q in range(QUARTERS):
        cols = slice(q * qw, (q + 1) * qw)
        part = b_f[:, cols]
        b_s[:, cols] = part.astype(BF)
        bt_s[cols, :] = part.T.astype(BF)

    def forward(g, carry):
        at = at_s[pl.ds(pl.multiple_of(g * gc, gc), gc), :]
        for q in range(QUARTERS):
            res = dot(at, b_s[:, q * qw : (q + 1) * qw]).astype(BF)
            for i in range(group):
                for d in range(DQ):
                    dd = q * DQ + d
                    ot_s[dd * C : (dd + 1) * C, i * tj : (i + 1) * tj] = res[
                        i * C : (i + 1) * C, d * tj : (d + 1) * tj
                    ]
        pre = dot(wt_s[...], ot_s[...]).T + bias
        sig = jax.nn.sigmoid(pre)
        first = pl.ds(pl.multiple_of(g * group, group), group)
        po_ref[first] = (pre * sig).astype(BF).reshape(group, tj, CZ)
        slope = sig * (1.0 + pre * (1.0 - sig))
        pg = pg_ref[first].reshape(gj, CZ).astype(F32)
        dpre = (pg * slope).astype(BF)
        dpre_f = dpre.astype(F32)
        bg_s[...] += jnp.sum(dpre_f.reshape(gj // 8, 8, CZ), axis=0)
        dt_s[g] = dpre_f.T.astype(BF)
        wg_s[...] += dot(ot_s[...], dpre)
        return carry

    lax.fori_loop(0, groups, forward, 0)

    bias_rows = jnp.broadcast_to(jnp.sum(bg_s[...], axis=0, keepdims=True), (8, CZ))
    for oo, xx, kk in every:
        first_row = row_of(oo, xx, kk) * wr
        for c in range(wr // C):
            wp[kk, xx, oo, c * C : (c + 1) * C, :] = wg_s[pl.ds(first_row // C + c, C, stride=C), :]
        wp[kk, xx, oo, wr : wr + 8, :] = bias_rows

    def weights():
        core = go(wp.at[1 - k], wc, wcs.at[0], wcr.at[0], cpeer)
        yield
        core.wait_recv()
        ws1[...] = wp[k, 1 - x] + wc[1 - x]
        xcopy = go(ws1, wx, wxs.at[0], wxr.at[0], xpeer)
        yield
        xcopy.wait_recv()
        ws2[...] = wp[k, x] + wc[x] + wx[...]
        zcopies = {
            t: go(ws2.at[flip(o, t)], wz.at[t], wzs.at[t], wzr.at[t], opeer[t])
            for t in range(1, n)
        }
        yield
        total = ws2[o]
        for t in range(1, n):
            zcopies[t].wait_recv()
            total = total + wz[t]
        wy[y] = total
        ycopies = [
            go(wy.at[y], wy.at[y], ysend.at[t], yrecv.at[t], ypeer[t]) for t in range(1, cn)
        ]
        yield
        for copy in ycopies:
            copy.wait_recv()
        total = wy[0]
        for yy in range(1, cn):
            total = total + wy[yy]
        total = total * (1.0 / first_total)
        wall[k, x, o] = jnp.concatenate([total, jnp.zeros((8, CZ), F32)], axis=0).astype(BF)
        yield from spread(n, ids, wall, spreads[6:])

    def rights(q):
        core = go(rp.at[q, 1 - k], rc.at[q], rcs.at[q], rcr.at[q], cpeer)
        yield
        core.wait_recv()
        rs1[q] = (rp[q, k, 1 - x].astype(F32) + rc[q, 1 - x].astype(F32)).astype(BF)
        xcopy = go(rs1.at[q], rx.at[q], rxs.at[q], rxr.at[q], xpeer)
        yield
        xcopy.wait_recv()
        for t in range(n - 1, -1, -1):
            at = flip(o, t)
            total = (
                rp[q, k, x, at].astype(F32) + rc[q, x, at].astype(F32) + rx[q, at].astype(F32)
            )
            if t:
                rs2[q, t] = total.astype(BF)
                zcopies[q, t] = go(
                    rs2.at[q, t], rz.at[q, t], rzs.at[q, t], rzr.at[q, t], opeer[t]
                )
        yield
        for t in range(1, n):
            zcopies[q, t].wait_recv()
            total = total + rz[q, t].astype(F32)
        for d in range(DQ):
            rfin[pl.ds(q * DQ + d, sr, stride=C), :] = total[:, d * tj : (d + 1) * tj]

    zcopies = {}
    steps = [weights()]
    next(steps[0])

    def advance():
        for step in steps:
            next(step, None)

    for q in range(QUARTERS):
        wq = w2_s[q * DQ * C : (q + 1) * DQ * C, :]

        def block(g, carry):
            res = dot(wq, dt_s[g]).astype(BF)
            for i in range(group):
                at = pl.ds(pl.multiple_of(g * gc + i * C, C), C)
                for d in range(DQ):
                    d_s[at, d * tj : (d + 1) * tj] = res[
                        d * C : (d + 1) * C, i * tj : (i + 1) * tj
                    ]
            return carry

        lax.fori_loop(0, groups, block, 0)
        right = dot(a_s[...], d_s[...])
        for oo, xx, kk in every:
            at = row_of(oo, xx, kk) * sr
            rp[q, kk, xx, oo] = right[at : at + sr].astype(BF)
        advance()
        steps.append(rights(q))
        next(steps[-1])
        part = dot(d_s[...], bt_s[q * qw : (q + 1) * qw, :])
        if q:
            lg_s[...] += part
        else:
            lg_s[...] = part
    for c in range(C):
        wide[pl.ds(c, S, stride=C), :] = lg_s[pl.ds(c, ti, stride=C), :].T * factor
    for yy in range(cn):
        lp[yy] = wide[yy * sc * C : (yy + 1) * sc * C, :].T.astype(BF)
    lefts = [
        go(lp.at[lax.rem(y + t, cn)], lbuf.at[t], lsend.at[t], lrecv.at[t], ypeer[t])
        for t in range(1, cn)
    ]
    for _ in range(3):
        advance()
    ro_ref[...] = rfin[...].T
    left = lp[y].astype(F32)
    for t in range(1, cn):
        lefts[t - 1].wait_recv()
        left = left + lbuf[t].astype(F32)
    lo_ref[...] = left
    for _ in steps[0]:
        pass
    for oo, xx, kk in every:
        at = row_of(oo, xx, kk) * wr
        wo_ref[at : at + wr, :] = wall[kk, xx, oo, 0:wr, :].astype(F32)
    bo_ref[...] = wall[0, 0, 0, wr : wr + 1, :].astype(F32)
    for copy in pending:
        copy.wait_send()


def on_device(left_act, right_act, out_weight, out_bias, pair_grad):
    n, cn = lax.axis_size("row") // 4, lax.axis_size("col")
    rows = 4 * n
    cc = C * C
    ti, tj = left_act.shape[0], right_act.shape[0]
    sr, wr = S // rows, cc // rows
    group = min(8, ti)
    dma = pltpu.SemaphoreType.DMA
    vmem = pl.BlockSpec(memory_space=pltpu.VMEM)
    qw = DQ * tj
    wb = wr + 8

    def buf(shape, dtype=BF):
        return pltpu.VMEM(shape, dtype)

    po, left, right, wgt, bia = pl.pallas_call(
        functools.partial(kernel, n, cn, ti, tj),
        out_shape=(
            jax.ShapeDtypeStruct(pair_grad.shape, BF),
            jax.ShapeDtypeStruct(left_act.shape, F32),
            jax.ShapeDtypeStruct(right_act.shape, F32),
            jax.ShapeDtypeStruct(out_weight.shape, F32),
            jax.ShapeDtypeStruct((1, CZ), F32),
        ),
        in_specs=[vmem] * 5,
        out_specs=(vmem,) * 5,
        scratch_shapes=[
            buf((cn,) + left_act.shape),
            buf((2, 2, n, sr, C * tj)),
            buf((sr * C, tj), F32),
            buf((S * C, ti), F32),
            buf((cc, CZ), F32),
            buf((cc, CZ)),
            buf((CZ, cc)),
            buf((ti * C, S), F32),
            buf((ti * C, S)),
            buf((S, ti * C)),
            buf((S, C * tj), F32),
            buf((S, C * tj)),
            buf((C * tj, S)),
            buf((cc, group * tj)),
            buf((ti // group, CZ, group * tj)),
            buf((ti * C, qw)),
            buf((cc, CZ), F32),
            buf((ti * C, S), F32),
            buf((8, CZ), F32),
            buf((QUARTERS, 2, 2, n, sr, qw)),
            buf((QUARTERS, 2, n, sr, qw)),
            buf((QUARTERS, n, sr, qw)),
            buf((QUARTERS, n, sr, qw)),
            buf((QUARTERS, n, sr, qw)),
            buf((QUARTERS, n, sr, qw)),
            buf((sr * C, tj), F32),
            buf((cn,) + left_act.shape),
            buf((cn,) + left_act.shape),
            buf((2, 2, n, wb, CZ), F32),
            buf((2, n, wb, CZ), F32),
            buf((n, wb, CZ), F32),
            buf((n, wb, CZ), F32),
            buf((n, wb, CZ), F32),
            buf((n, wb, CZ), F32),
            buf((cn, wb, CZ), F32),
            buf((2, 2, n, wr + 16, CZ)),
        ]
        + [dma((cn,))] * 6
        + [dma((QUARTERS,))] * 4
        + [dma((QUARTERS, n))] * 2
        + [dma((1,))] * 4
        + [dma((n,))] * 2
        + spread_sems(n)
        + spread_sems(n),
        compiler_params=pltpu.CompilerParams(
            collective_id=0, has_side_effects=True, vmem_limit_bytes=60 * 1024 * 1024
        ),
        name="pairs",
    )(left_act, right_act, out_weight, out_bias.reshape(1, CZ), pair_grad)
    return (po, left, right, wgt, bia.reshape(CZ))


def solution(mesh):
    in_specs = (P("row", "col"), P("col", "row"), P(), P(), P("row", "col", None))
    out_specs = (P("row", "col", None), P("row", "col"), P("col", "row"), P(), P())
    return jax.shard_map(
        on_device, mesh=mesh, in_specs=in_specs, out_specs=out_specs, check_vma=False
    )
```

```python
import functools

import jax
import jax.numpy as jnp
from jax import lax
from jax.experimental import pallas as pl
from jax.experimental.pallas import tpu as pltpu
from jax.sharding import PartitionSpec as P

S = 128
C = 32
CZ = 128
MESH = pl.DeviceIdType.MESH
BF = jnp.bfloat16
F32 = jnp.float32
DQ = 8
PAD = 16
QUARTERS = C // DQ


def dot(a, b):
    return jnp.dot(a, b, preferred_element_type=F32)


def flip(o, t):
    out, bit = 0, 1
    while bit <= t:
        here = (o // bit) % 2
        out = out + bit * ((1 - here) if (t & bit) else here)
        bit *= 2
    return out + (o // bit) * bit


def row_of(o, x, k):
    return o * 4 + x * 2 + k


def remote(src, dst, send, recv, peer):
    return pltpu.make_async_remote_copy(
        src_ref=src, dst_ref=dst, send_sem=send, recv_sem=recv, device_id=peer, device_id_type=MESH
    )


def spread(n, ids, buf, sems):
    o, x, k, y = ids
    zs, zr, xs, xr, cs, cr = sems
    started = []

    def send(slot, ss, rs, peer):
        copy = remote(buf.at[slot], buf.at[slot], ss, rs, peer)
        copy.start()
        started.append(copy)
        return copy

    xpeer, cpeer = (row_of(o, 1 - x, k), y), (row_of(o, x, 1 - k), y)
    own = (k, x, o)
    zc = {t: send(own, zs.at[t], zr.at[t], (row_of(flip(o, t), x, k), y)) for t in range(1, n)}
    xc = [send(own, xs.at[0], xr.at[0], xpeer)]
    cc = [send(own, cs.at[0], cr.at[0], cpeer)]
    yield
    for t in range(1, n):
        zc[t].wait_recv()
        slot = (k, x, flip(o, t))
        xc.append(send(slot, xs.at[t], xr.at[t], xpeer))
        cc.append(send(slot, cs.at[t], cr.at[t], cpeer))
    yield
    for t in range(n):
        xc[t].wait_recv()
        slot = (k, 1 - x, flip(o, t))
        cc.append(send(slot, cs.at[n + t], cr.at[n + t], cpeer))
    yield
    for copy in cc:
        copy.wait_recv()
    for copy in started:
        copy.wait_send()


def spread_sems(n):
    dma = pltpu.SemaphoreType.DMA
    return [dma((n,)), dma((n,)), dma((n,)), dma((n,)), dma((2 * n,)), dma((2 * n,))]


def kernel(
    n, cn, ti, tj, left_ref, right_ref, w_ref, bias_ref, pg_ref,
    po_ref, lo_ref, ro_ref, wo_ref, bo_ref,
    a_all, b_all, b_t, wide, w_f, w2_s, wt_s, at_f, at_s, a_s, b_f, b_s, bt_s,
    ot_s, dt_s, d_s, wg_s, lg_s, bg_s,
    rp, rc, rs1, rx, rs2, rz, rfin, lp, lbuf, wp, wc, ws1, wx, ws2, wz, wy, wall,
    asend, arecv, lsend, lrecv, ysend, yrecv,
    rcs, rcr, rxs, rxr, rzs, rzr, wcs, wcr, wxs, wxr, wzs, wzr, *spreads,
):
    r = lax.axis_index("row")
    o, x, k, y = r // 4, (r // 2) % 2, r % 2, lax.axis_index("col")
    ids = (o, x, k, y)
    xpeer, cpeer = (row_of(o, 1 - x, k), y), (row_of(o, x, 1 - k), y)
    opeer = {t: (row_of(flip(o, t), x, k), y) for t in range(1, n)}
    ypeer = {t: (r, lax.rem(y + t, cn)) for t in range(1, cn)}
    factor = 1.0 / S
    cc = C * C
    rows = 4 * n
    sr, sc, wr = S // rows, S // cn, cc // rows
    first_total = ti * rows
    group = min(8, ti)
    gc, gj = group * C, group * tj
    groups = ti // group
    qw = DQ * tj
    every = [(oo, xx, kk) for oo in range(n) for xx in range(2) for kk in range(2)]
    pending = []

    def go(src, dst, ss, rs, peer):
        copy = remote(src, dst, ss, rs, peer)
        copy.start()
        pending.append(copy)
        return copy

    barrier = pltpu.get_barrier_semaphore()
    peers = list(opeer.values()) + [xpeer, cpeer] + list(ypeer.values())
    for peer in peers:
        pl.semaphore_signal(barrier, inc=1, device_id=peer, device_id_type=MESH)
    b_t[...] = right_ref[...].astype(F32).T
    for d in range(C):
        b_all[k, x, o, :, d * tj : (d + 1) * tj] = b_t[pl.ds(d, sr, stride=C), :].astype(BF)
    pl.semaphore_wait(barrier, len(peers))
    ring = spread(n, ids, b_all, spreads[:6])
    next(ring)
    firsts = [
        go(left_ref, a_all.at[y], asend.at[t], arecv.at[t], ypeer[t]) for t in range(1, cn)
    ]
    a_all[y] = left_ref[...]
    w_f[...] = w_ref[...].astype(F32)
    for d in range(C):
        w2_s[d * C : (d + 1) * C, :] = w_f[pl.ds(d, C, stride=C), :].astype(BF)
    next(ring)
    wt_s[...] = w2_s[...].astype(F32).T.astype(BF)
    wg_s[...] = jnp.zeros_like(wg_s)
    bg_s[...] = jnp.zeros_like(bg_s)
    bias = bias_ref[...]
    for copy in firsts:
        copy.wait_recv()
    next(ring)
    for yy in range(cn):
        wide[yy * sc * C : (yy + 1) * sc * C, :] = a_all[yy].astype(F32).T
    for c in range(C):
        at_f[pl.ds(c, ti, stride=C), :] = wide[pl.ds(c, S, stride=C), :].T * factor
    at_s[...] = at_f[...].astype(BF)
    a_s[...] = at_f[...].T.astype(BF)
    for _ in ring:
        pass
    for oo, xx, kk in every:
        b_f[pl.ds(row_of(oo, xx, kk) * sr, sr), :] = b_all[kk, xx, oo].astype(F32)
    for q in range(QUARTERS):
        cols = slice(q * qw, (q + 1) * qw)
        part = b_f[:, cols]
        b_s[:, cols] = part.astype(BF)
        bt_s[cols, :] = part.T.astype(BF)

    def forward(g, carry):
        at = at_s[pl.ds(pl.multiple_of(g * gc, gc), gc), :]
        for q in range(QUARTERS):
            res = dot(at, b_s[:, q * qw : (q + 1) * qw]).astype(BF)
            for i in range(group):
                for d in range(DQ):
                    dd = q * DQ + d
                    ot_s[dd * C : (dd + 1) * C, i * tj : (i + 1) * tj] = res[
                        i * C : (i + 1) * C, d * tj : (d + 1) * tj
                    ]
        pre = dot(wt_s[...], ot_s[...]).T + bias
        sig = jax.nn.sigmoid(pre)
        first = pl.ds(pl.multiple_of(g * group, group), group)
        po_ref[first] = (pre * sig).astype(BF).reshape(group, tj, CZ)
        slope = sig * (1.0 + pre * (1.0 - sig))
        pg = pg_ref[first].reshape(gj, CZ).astype(F32)
        dpre = (pg * slope).astype(BF)
        dpre_f = dpre.astype(F32)
        bg_s[...] += jnp.sum(dpre_f.reshape(gj // 8, 8, CZ), axis=0)
        dt_s[g] = dpre_f.T.astype(BF)
        wg_s[...] += dot(ot_s[...], dpre)
        return carry

    lax.fori_loop(0, groups, forward, 0)

    bias_rows = jnp.broadcast_to(jnp.sum(bg_s[...], axis=0, keepdims=True), (PAD, CZ))
    for oo, xx, kk in every:
        first_row = row_of(oo, xx, kk) * wr
        for c in range(wr // C):
            wp[kk, xx, oo, c * C : (c + 1) * C, :] = wg_s[pl.ds(first_row // C + c, C, stride=C), :]
        wp[kk, xx, oo, wr : wr + PAD, :] = bias_rows

    def weights():
        core = go(wp.at[1 - k], wc, wcs.at[0], wcr.at[0], cpeer)
        yield
        core.wait_recv()
        ws1[...] = (wp[k, 1 - x] + wc[1 - x]).astype(BF)
        xcopy = go(ws1, wx, wxs.at[0], wxr.at[0], xpeer)
        yield
        xcopy.wait_recv()
        for t in range(n - 1, -1, -1):
            at = flip(o, t)
            total = wp[k, x, at] + wc[x, at] + wx[at].astype(F32)
            if t:
                ws2[t] = total.astype(BF)
                wcopies[t] = go(ws2.at[t], wz.at[t], wzs.at[t], wzr.at[t], opeer[t])
        yield
        for t in range(1, n):
            wcopies[t].wait_recv()
            total = total + wz[t].astype(F32)
        wy[y] = total
        ycopies = [
            go(wy.at[y], wy.at[y], ysend.at[t], yrecv.at[t], ypeer[t]) for t in range(1, cn)
        ]
        yield
        for copy in ycopies:
            copy.wait_recv()
        total = wy[0]
        for yy in range(1, cn):
            total = total + wy[yy]
        total = total * (1.0 / first_total)
        wall[k, x, o] = total.astype(BF)
        yield from spread(n, ids, wall, spreads[6:])

    def rights(q):
        core = go(rp.at[q, 1 - k], rc.at[q], rcs.at[q], rcr.at[q], cpeer)
        yield
        core.wait_recv()
        rs1[q] = (rp[q, k, 1 - x].astype(F32) + rc[q, 1 - x].astype(F32)).astype(BF)
        xcopy = go(rs1.at[q], rx.at[q], rxs.at[q], rxr.at[q], xpeer)
        yield
        xcopy.wait_recv()
        for t in range(n - 1, -1, -1):
            at = flip(o, t)
            total = (
                rp[q, k, x, at].astype(F32) + rc[q, x, at].astype(F32) + rx[q, at].astype(F32)
            )
            if t:
                rs2[q, t] = total.astype(BF)
                zcopies[q, t] = go(
                    rs2.at[q, t], rz.at[q, t], rzs.at[q, t], rzr.at[q, t], opeer[t]
                )
        yield
        for t in range(1, n):
            zcopies[q, t].wait_recv()
            total = total + rz[q, t].astype(F32)
        for d in range(DQ):
            rfin[pl.ds(q * DQ + d, sr, stride=C), :] = total[:, d * tj : (d + 1) * tj]

    zcopies, wcopies = {}, {}
    steps = [weights()]
    next(steps[0])

    def advance():
        for step in steps:
            next(step, None)

    for q in range(QUARTERS):
        wq = w2_s[q * DQ * C : (q + 1) * DQ * C, :]

        def block(g, carry):
            res = dot(wq, dt_s[g]).astype(BF)
            for i in range(group):
                at = pl.ds(pl.multiple_of(g * gc + i * C, C), C)
                for d in range(DQ):
                    d_s[at, d * tj : (d + 1) * tj] = res[
                        d * C : (d + 1) * C, i * tj : (i + 1) * tj
                    ]
            return carry

        lax.fori_loop(0, groups, block, 0)
        right = dot(a_s[...], d_s[...])
        for oo, xx, kk in every:
            at = row_of(oo, xx, kk) * sr
            rp[q, kk, xx, oo] = right[at : at + sr].astype(BF)
        advance()
        steps.append(rights(q))
        next(steps[-1])
        part = dot(d_s[...], bt_s[q * qw : (q + 1) * qw, :])
        if q:
            lg_s[...] += part
        else:
            lg_s[...] = part
    for c in range(C):
        if c == C // 2:
            advance()
        wide[pl.ds(c, S, stride=C), :] = lg_s[pl.ds(c, ti, stride=C), :].T * factor
    for yy in range(cn):
        lp[yy] = wide[yy * sc * C : (yy + 1) * sc * C, :].T.astype(BF)
    lefts = [
        go(lp.at[lax.rem(y + t, cn)], lbuf.at[t], lsend.at[t], lrecv.at[t], ypeer[t])
        for t in range(1, cn)
    ]
    for _ in range(2):
        advance()
    ro_ref[...] = rfin[...].T
    left = lp[y].astype(F32)
    for t in range(1, cn):
        lefts[t - 1].wait_recv()
        left = left + lbuf[t].astype(F32)
    lo_ref[...] = left
    for _ in steps[0]:
        pass
    for oo, xx, kk in every:
        at = row_of(oo, xx, kk) * wr
        wo_ref[at : at + wr, :] = wall[kk, xx, oo, 0:wr, :].astype(F32)
    bo_ref[...] = wall[0, 0, 0, wr : wr + 1, :].astype(F32)
    for copy in pending:
        copy.wait_send()


def on_device(left_act, right_act, out_weight, out_bias, pair_grad):
    n, cn = lax.axis_size("row") // 4, lax.axis_size("col")
    rows = 4 * n
    cc = C * C
    ti, tj = left_act.shape[0], right_act.shape[0]
    sr, wr = S // rows, cc // rows
    group = min(8, ti)
    dma = pltpu.SemaphoreType.DMA
    vmem = pl.BlockSpec(memory_space=pltpu.VMEM)
    qw = DQ * tj
    wb = wr + PAD

    def buf(shape, dtype=BF):
        return pltpu.VMEM(shape, dtype)

    po, left, right, wgt, bia = pl.pallas_call(
        functools.partial(kernel, n, cn, ti, tj),
        out_shape=(
            buf(pair_grad.shape, BF),
            buf(left_act.shape, F32),
            buf(right_act.shape, F32),
            buf(out_weight.shape, F32),
            buf((1, CZ), F32),
        ),
        in_specs=[vmem] * 5,
        out_specs=(vmem,) * 5,
        scratch_shapes=[
            buf((cn,) + left_act.shape),
            buf((2, 2, n, sr, C * tj)),
            buf((sr * C, tj), F32),
            buf((S * C, ti), F32),
            buf((cc, CZ), F32),
            buf((cc, CZ)),
            buf((CZ, cc)),
            buf((ti * C, S), F32),
            buf((ti * C, S)),
            buf((S, ti * C)),
            buf((S, C * tj), F32),
            buf((S, C * tj)),
            buf((C * tj, S)),
            buf((cc, group * tj)),
            buf((ti // group, CZ, group * tj)),
            buf((ti * C, qw)),
            buf((cc, CZ), F32),
            buf((ti * C, S), F32),
            buf((8, CZ), F32),
            buf((QUARTERS, 2, 2, n, sr, qw)),
            buf((QUARTERS, 2, n, sr, qw)),
            buf((QUARTERS, n, sr, qw)),
            buf((QUARTERS, n, sr, qw)),
            buf((QUARTERS, n, sr, qw)),
            buf((QUARTERS, n, sr, qw)),
            buf((sr * C, tj), F32),
            buf((cn,) + left_act.shape),
            buf((cn,) + left_act.shape),
            buf((2, 2, n, wb, CZ), F32),
            buf((2, n, wb, CZ), F32),
            buf((n, wb, CZ)),
            buf((n, wb, CZ)),
            buf((n, wb, CZ)),
            buf((n, wb, CZ)),
            buf((cn, wb, CZ), F32),
            buf((2, 2, n, wb, CZ)),
        ]
        + [dma((cn,))] * 6
        + [dma((QUARTERS,))] * 4
        + [dma((QUARTERS, n))] * 2
        + [dma((1,))] * 4
        + [dma((n,))] * 2
        + spread_sems(n)
        + spread_sems(n),
        compiler_params=pltpu.CompilerParams(
            collective_id=0, has_side_effects=True, vmem_limit_bytes=40 * 1024 * 1024
        ),
        name="pairs",
    )(left_act, right_act, out_weight, out_bias.reshape(1, CZ), pair_grad)
    return (po, left, right, wgt, bia.reshape(CZ))


def solution(mesh):
    in_specs = (P("row", "col"), P("col", "row"), P(), P(), P("row", "col", None))
    out_specs = (P("row", "col", None), P("row", "col"), P("col", "row"), P(), P())
    return jax.shard_map(
        on_device, mesh=mesh, in_specs=in_specs, out_specs=out_specs, check_vma=False
    )
```

```python
import functools

import jax
import jax.numpy as jnp
from jax import lax
from jax.experimental import pallas as pl
from jax.experimental.pallas import tpu as pltpu
from jax.sharding import PartitionSpec as P

S = 128
C = 32
CZ = 128
MESH = pl.DeviceIdType.MESH
BF = jnp.bfloat16
F32 = jnp.float32
DQ = 8
PAD = 16
QUARTERS = C // DQ


def dot(a, b):
    return jnp.dot(a, b, preferred_element_type=F32)


def flip(o, t):
    out, bit = 0, 1
    while bit <= t:
        here = (o // bit) % 2
        out = out + bit * ((1 - here) if (t & bit) else here)
        bit *= 2
    return out + (o // bit) * bit


def row_of(o, x, k):
    return o * 4 + x * 2 + k


def remote(src, dst, send, recv, peer):
    return pltpu.make_async_remote_copy(
        src_ref=src, dst_ref=dst, send_sem=send, recv_sem=recv, device_id=peer, device_id_type=MESH
    )


def spread(n, ids, buf, sems):
    o, x, k, y = ids
    zs, zr, xs, xr, cs, cr = sems
    started = []

    def send(slot, ss, rs, peer):
        copy = remote(buf.at[slot], buf.at[slot], ss, rs, peer)
        copy.start()
        started.append(copy)
        return copy

    xpeer, cpeer = (row_of(o, 1 - x, k), y), (row_of(o, x, 1 - k), y)
    own = (k, x, o)
    zc = {t: send(own, zs.at[t], zr.at[t], (row_of(flip(o, t), x, k), y)) for t in range(1, n)}
    xc = [send(own, xs.at[0], xr.at[0], xpeer)]
    cc = [send(own, cs.at[0], cr.at[0], cpeer)]
    yield
    for t in range(1, n):
        zc[t].wait_recv()
        slot = (k, x, flip(o, t))
        xc.append(send(slot, xs.at[t], xr.at[t], xpeer))
        cc.append(send(slot, cs.at[t], cr.at[t], cpeer))
    yield
    for t in range(n):
        xc[t].wait_recv()
        slot = (k, 1 - x, flip(o, t))
        cc.append(send(slot, cs.at[n + t], cr.at[n + t], cpeer))
    yield
    for copy in cc:
        copy.wait_recv()
    for copy in started:
        copy.wait_send()


def spread_sems(n):
    dma = pltpu.SemaphoreType.DMA
    return [dma((n,)), dma((n,)), dma((n,)), dma((n,)), dma((2 * n,)), dma((2 * n,))]


def kernel(
    n, cn, ti, tj, left_ref, right_ref, w_ref, bias_ref, pg_ref,
    po_ref, lo_ref, ro_ref, wo_ref, bo_ref,
    right_v, w_v, pg_v, isem, a_all, b_all, b_t, wide, w_f, w2_s, wt_s, at_f, at_s, a_s, b_f, b_s, bt_s,
    ot_s, dt_s, d_s, wg_s, lg_s, bg_s,
    rp, rc, rs1, rx, rs2, rz, rfin, lp, lbuf, wp, wc, ws1, wx, ws2, wz, wy, wall,
    asend, arecv, lsend, lrecv, ysend, yrecv,
    rcs, rcr, rxs, rxr, rzs, rzr, wcs, wcr, wxs, wxr, wzs, wzr, *spreads,
):
    r = lax.axis_index("row")
    o, x, k, y = r // 4, (r // 2) % 2, r % 2, lax.axis_index("col")
    ids = (o, x, k, y)
    xpeer, cpeer = (row_of(o, 1 - x, k), y), (row_of(o, x, 1 - k), y)
    opeer = {t: (row_of(flip(o, t), x, k), y) for t in range(1, n)}
    ypeer = {t: (r, lax.rem(y + t, cn)) for t in range(1, cn)}
    factor = 1.0 / S
    cc = C * C
    rows = 4 * n
    sr, sc, wr = S // rows, S // cn, cc // rows
    first_total = ti * rows
    group = min(8, ti)
    gc, gj = group * C, group * tj
    groups = ti // group
    qw = DQ * tj
    every = [(oo, xx, kk) for oo in range(n) for xx in range(2) for kk in range(2)]
    pending = []

    def go(src, dst, ss, rs, peer):
        copy = remote(src, dst, ss, rs, peer)
        copy.start()
        pending.append(copy)
        return copy

    loads = [
        pltpu.make_async_copy(right_ref, right_v, isem.at[0]),
        pltpu.make_async_copy(w_ref, w_v, isem.at[1]),
        pltpu.make_async_copy(left_ref, a_all.at[y], isem.at[2]),
        pltpu.make_async_copy(pg_ref, pg_v, isem.at[3]),
    ]
    for load in loads:
        load.start()
    barrier = pltpu.get_barrier_semaphore()
    peers = list(opeer.values()) + [xpeer, cpeer] + list(ypeer.values())
    for peer in peers:
        pl.semaphore_signal(barrier, inc=1, device_id=peer, device_id_type=MESH)
    loads[0].wait()
    b_t[...] = right_v[...].astype(F32).T
    for d in range(C):
        b_all[k, x, o, :, d * tj : (d + 1) * tj] = b_t[pl.ds(d, sr, stride=C), :].astype(BF)
    pl.semaphore_wait(barrier, len(peers))
    ring = spread(n, ids, b_all, spreads[:6])
    next(ring)
    firsts = [
        go(left_ref, a_all.at[y], asend.at[t], arecv.at[t], ypeer[t]) for t in range(1, cn)
    ]
    loads[1].wait()
    w_f[...] = w_v[...].astype(F32)
    for d in range(C):
        w2_s[d * C : (d + 1) * C, :] = w_f[pl.ds(d, C, stride=C), :].astype(BF)
    next(ring)
    wt_s[...] = w2_s[...].astype(F32).T.astype(BF)
    wg_s[...] = jnp.zeros_like(wg_s)
    bg_s[...] = jnp.zeros_like(bg_s)
    bias = bias_ref[...]
    loads[2].wait()
    for copy in firsts:
        copy.wait_recv()
    next(ring)
    for yy in range(cn):
        wide[yy * sc * C : (yy + 1) * sc * C, :] = a_all[yy].astype(F32).T
    for c in range(C):
        at_f[pl.ds(c, ti, stride=C), :] = wide[pl.ds(c, S, stride=C), :].T * factor
    at_s[...] = at_f[...].astype(BF)
    a_s[...] = at_f[...].T.astype(BF)
    for _ in ring:
        pass
    for oo, xx, kk in every:
        b_f[pl.ds(row_of(oo, xx, kk) * sr, sr), :] = b_all[kk, xx, oo].astype(F32)
    for q in range(QUARTERS):
        cols = slice(q * qw, (q + 1) * qw)
        part = b_f[:, cols]
        b_s[:, cols] = part.astype(BF)
        bt_s[cols, :] = part.T.astype(BF)

    loads[3].wait()

    def forward(g, carry):
        at = at_s[pl.ds(pl.multiple_of(g * gc, gc), gc), :]
        for q in range(QUARTERS):
            res = dot(at, b_s[:, q * qw : (q + 1) * qw]).astype(BF)
            for i in range(group):
                for d in range(DQ):
                    dd = q * DQ + d
                    ot_s[dd * C : (dd + 1) * C, i * tj : (i + 1) * tj] = res[
                        i * C : (i + 1) * C, d * tj : (d + 1) * tj
                    ]
        pre = dot(wt_s[...], ot_s[...]).T + bias
        sig = jax.nn.sigmoid(pre)
        first = pl.ds(pl.multiple_of(g * group, group), group)
        po_ref[first] = (pre * sig).astype(BF).reshape(group, tj, CZ)
        slope = sig * (1.0 + pre * (1.0 - sig))
        pg = pg_v[first].reshape(gj, CZ).astype(F32)
        dpre = (pg * slope).astype(BF)
        dpre_f = dpre.astype(F32)
        bg_s[...] += jnp.sum(dpre_f.reshape(gj // 8, 8, CZ), axis=0)
        dt_s[g] = dpre_f.T.astype(BF)
        wg_s[...] += dot(ot_s[...], dpre)
        return carry

    lax.fori_loop(0, groups, forward, 0)

    bias_rows = jnp.broadcast_to(jnp.sum(bg_s[...], axis=0, keepdims=True), (PAD, CZ))
    for oo, xx, kk in every:
        first_row = row_of(oo, xx, kk) * wr
        for c in range(wr // C):
            wp[kk, xx, oo, c * C : (c + 1) * C, :] = wg_s[pl.ds(first_row // C + c, C, stride=C), :]
        wp[kk, xx, oo, wr : wr + PAD, :] = bias_rows

    def weights():
        core = go(wp.at[1 - k], wc, wcs.at[0], wcr.at[0], cpeer)
        yield
        core.wait_recv()
        ws1[...] = (wp[k, 1 - x] + wc[1 - x]).astype(BF)
        xcopy = go(ws1, wx, wxs.at[0], wxr.at[0], xpeer)
        yield
        xcopy.wait_recv()
        for t in range(n - 1, -1, -1):
            at = flip(o, t)
            total = wp[k, x, at] + wc[x, at] + wx[at].astype(F32)
            if t:
                ws2[t] = total.astype(BF)
                wcopies[t] = go(ws2.at[t], wz.at[t], wzs.at[t], wzr.at[t], opeer[t])
        yield
        for t in range(1, n):
            wcopies[t].wait_recv()
            total = total + wz[t].astype(F32)
        wy[y] = total
        ycopies = [
            go(wy.at[y], wy.at[y], ysend.at[t], yrecv.at[t], ypeer[t]) for t in range(1, cn)
        ]
        yield
        for copy in ycopies:
            copy.wait_recv()
        total = wy[0]
        for yy in range(1, cn):
            total = total + wy[yy]
        total = total * (1.0 / first_total)
        wall[k, x, o] = total.astype(BF)
        yield from spread(n, ids, wall, spreads[6:])

    def rights(q):
        core = go(rp.at[q, 1 - k], rc.at[q], rcs.at[q], rcr.at[q], cpeer)
        yield
        core.wait_recv()
        rs1[q] = (rp[q, k, 1 - x].astype(F32) + rc[q, 1 - x].astype(F32)).astype(BF)
        xcopy = go(rs1.at[q], rx.at[q], rxs.at[q], rxr.at[q], xpeer)
        yield
        xcopy.wait_recv()
        for t in range(n - 1, -1, -1):
            at = flip(o, t)
            total = (
                rp[q, k, x, at].astype(F32) + rc[q, x, at].astype(F32) + rx[q, at].astype(F32)
            )
            if t:
                rs2[q, t] = total.astype(BF)
                zcopies[q, t] = go(
                    rs2.at[q, t], rz.at[q, t], rzs.at[q, t], rzr.at[q, t], opeer[t]
                )
        yield
        for t in range(1, n):
            zcopies[q, t].wait_recv()
            total = total + rz[q, t].astype(F32)
        for d in range(DQ):
            rfin[pl.ds(q * DQ + d, sr, stride=C), :] = total[:, d * tj : (d + 1) * tj]

    zcopies, wcopies = {}, {}
    steps = [weights()]
    next(steps[0])

    def advance():
        for step in steps[1:] + steps[:1]:
            next(step, None)

    for q in range(QUARTERS):
        wq = w2_s[q * DQ * C : (q + 1) * DQ * C, :]

        def block(g, carry):
            res = dot(wq, dt_s[g]).astype(BF)
            for i in range(group):
                at = pl.ds(pl.multiple_of(g * gc + i * C, C), C)
                for d in range(DQ):
                    d_s[at, d * tj : (d + 1) * tj] = res[
                        d * C : (d + 1) * C, i * tj : (i + 1) * tj
                    ]
            return carry

        lax.fori_loop(0, groups, block, 0)
        right = dot(a_s[...], d_s[...])
        for oo, xx, kk in every:
            at = row_of(oo, xx, kk) * sr
            rp[q, kk, xx, oo] = right[at : at + sr].astype(BF)
        advance()
        steps.append(rights(q))
        next(steps[-1])
        part = dot(d_s[...], bt_s[q * qw : (q + 1) * qw, :])
        if q:
            lg_s[...] += part
        else:
            lg_s[...] = part
    for c in range(C):
        if c == C // 2:
            advance()
        wide[pl.ds(c, S, stride=C), :] = lg_s[pl.ds(c, ti, stride=C), :].T * factor
    for yy in range(cn):
        lp[yy] = wide[yy * sc * C : (yy + 1) * sc * C, :].T.astype(BF)
    lefts = [
        go(lp.at[lax.rem(y + t, cn)], lbuf.at[t], lsend.at[t], lrecv.at[t], ypeer[t])
        for t in range(1, cn)
    ]
    for _ in range(2):
        advance()
    ro_ref[...] = rfin[...].T
    left = lp[y].astype(F32)
    for t in range(1, cn):
        lefts[t - 1].wait_recv()
        left = left + lbuf[t].astype(F32)
    lo_ref[...] = left
    for _ in steps[0]:
        pass
    for oo, xx, kk in every:
        at = row_of(oo, xx, kk) * wr
        wo_ref[at : at + wr, :] = wall[kk, xx, oo, 0:wr, :].astype(F32)
    bo_ref[...] = wall[0, 0, 0, wr : wr + 1, :].astype(F32)
    for copy in pending:
        copy.wait_send()


def on_device(left_act, right_act, out_weight, out_bias, pair_grad):
    n, cn = lax.axis_size("row") // 4, lax.axis_size("col")
    rows = 4 * n
    cc = C * C
    ti, tj = left_act.shape[0], right_act.shape[0]
    sr, wr = S // rows, cc // rows
    group = min(8, ti)
    dma = pltpu.SemaphoreType.DMA
    vmem = pl.BlockSpec(memory_space=pltpu.VMEM)
    hbm = pl.BlockSpec(memory_space=pltpu.HBM)
    qw = DQ * tj
    wb = wr + PAD

    def buf(shape, dtype=BF):
        return pltpu.VMEM(shape, dtype)

    po, left, right, wgt, bia = pl.pallas_call(
        functools.partial(kernel, n, cn, ti, tj),
        out_shape=(
            buf(pair_grad.shape, BF),
            buf(left_act.shape, F32),
            buf(right_act.shape, F32),
            buf(out_weight.shape, F32),
            buf((1, CZ), F32),
        ),
        in_specs=[hbm, hbm, hbm, vmem, hbm],
        out_specs=(vmem,) * 5,
        scratch_shapes=[
            buf(right_act.shape),
            buf(out_weight.shape),
            buf(pair_grad.shape),
            dma((4,)),
            buf((cn,) + left_act.shape),
            buf((2, 2, n, sr, C * tj)),
            buf((sr * C, tj), F32),
            buf((S * C, ti), F32),
            buf((cc, CZ), F32),
            buf((cc, CZ)),
            buf((CZ, cc)),
            buf((ti * C, S), F32),
            buf((ti * C, S)),
            buf((S, ti * C)),
            buf((S, C * tj), F32),
            buf((S, C * tj)),
            buf((C * tj, S)),
            buf((cc, group * tj)),
            buf((ti // group, CZ, group * tj)),
            buf((ti * C, qw)),
            buf((cc, CZ), F32),
            buf((ti * C, S), F32),
            buf((8, CZ), F32),
            buf((QUARTERS, 2, 2, n, sr, qw)),
            buf((QUARTERS, 2, n, sr, qw)),
            buf((QUARTERS, n, sr, qw)),
            buf((QUARTERS, n, sr, qw)),
            buf((QUARTERS, n, sr, qw)),
            buf((QUARTERS, n, sr, qw)),
            buf((sr * C, tj), F32),
            buf((cn,) + left_act.shape),
            buf((cn,) + left_act.shape),
            buf((2, 2, n, wb, CZ), F32),
            buf((2, n, wb, CZ), F32),
            buf((n, wb, CZ)),
            buf((n, wb, CZ)),
            buf((n, wb, CZ)),
            buf((n, wb, CZ)),
            buf((cn, wb, CZ), F32),
            buf((2, 2, n, wb, CZ)),
        ]
        + [dma((cn,))] * 6
        + [dma((QUARTERS,))] * 4
        + [dma((QUARTERS, n))] * 2
        + [dma((1,))] * 4
        + [dma((n,))] * 2
        + spread_sems(n)
        + spread_sems(n),
        compiler_params=pltpu.CompilerParams(
            collective_id=0, has_side_effects=True, vmem_limit_bytes=40 * 1024 * 1024
        ),
        name="pairs",
    )(left_act, right_act, out_weight, out_bias.reshape(1, CZ), pair_grad)
    return (po, left, right, wgt, bia.reshape(CZ))


def solution(mesh):
    in_specs = (P("row", "col"), P("col", "row"), P(), P(), P("row", "col", None))
    out_specs = (P("row", "col", None), P("row", "col"), P("col", "row"), P(), P())
    return jax.shard_map(
        on_device, mesh=mesh, in_specs=in_specs, out_specs=out_specs, check_vma=False
    )
```
